32 devices in a mesh: gx: 4 (over y, x), gy: 2 (over core), gz: 4 (over z).
Axes of the slice: x: 2, y: 2, z: 4, core: 2. Of those that a mesh axis runs over, the one named last changes fastest.
Arguments:
- positions: float32 [3, 4, 2, 4, 128], P(None, 'gx', 'gy', 'gz'), may hold values from 0 to 1
- basis: float32 [30, 3, 4, 2, 4, 128], P(None, None, 'gx', 'gy', 'gz'), may hold values from -10 to 10, as said below
- neighbours: int32 [4, 2, 4, 128, 128], P('gx', 'gy', 'gz'), may hold values from 0 to 511
- used_count: int32 [4, 2, 4, 128], P('gx', 'gy', 'gz'), may hold values from 42 to 128
- kinds: int32 [4, 2, 4, 128], P('gx', 'gy', 'gz'), may hold values from 0 to 1
- map_x: int32 [4, 2, 4, 2, 64], P('gx', 'gy', 'gz'), may hold values from 0 to 127
- map_y: int32 [4, 2, 4, 2, 64], P('gx', 'gy', 'gz'), may hold values from 0 to 255
- map_z: int32 [4, 2, 4, 2, 64], P('gx', 'gy', 'gz'), may hold values from 0 to 383
- table: float32 [2, 16, 100], replicated, may hold values from -6 to 6
- fit_w1: float32 [1600, 240], replicated, may hold values from -0.15625 to 0.15625
- fit_b1: float32 [240], replicated, may hold values from -3 to 3
- fit_w2: float32 [240, 240], replicated, may hold values from -0.375 to 0.375
- fit_b2: float32 [240], replicated, may hold values from -3 to 3
- fit_out: float32 [240], replicated, may hold values from -0.375 to 0.375
Outputs:
- next_vector: float32 [3, 4, 2, 4, 128], P(None, 'gx', 'gy', 'gz')
- correlations: float32 [30], replicated
- vector_norm: float32 [], replicated
The draws below stay inside these ranges and needn't reach their ends.
Inputs may be any that keep to these rules, and one draw needn't show every extreme that they name: `basis`: entries of order one; the stored vectors' magnitude varies from brick to brick.
All inputs are finite; a program needn't handle non-finite values.
Results may differ from the reference program's by a relative error of at most 0.0003.
Values sent between devices are 32-bit elements; how exact they have to be, the bound alone decides.
A program may use at most 64 MiB of HBM per device.

```python
import jax
import jax.numpy as jnp
from jax import lax

ATOMS_DEV = 128
NNEI = 128
NBASIS = 16
M1 = 100
M2 = 16
FIT = 240
NTYPES = 2
KVEC = 30
GRID_X = 4
GRID_Y = 2
GRID_Z = 4
GHOST = 64
EXT = 512


def draw_basis(key, part):
    first_key, second_key, third_key = jax.random.split(jax.random.fold_in(key, 17), 3)
    shape = (KVEC, 3, GRID_X, GRID_Y, GRID_Z, ATOMS_DEV)
    bricks = GRID_X * GRID_Y * GRID_Z
    order = jnp.arange(bricks, dtype=jnp.float32).reshape(1, 1, GRID_X, GRID_Y, GRID_Z, 1)
    fraction = order / max(bricks - 1, 1)
    private = jax.random.truncated_normal(first_key, -3.0, 3.0, shape, jnp.float32)
    shared = jax.random.truncated_normal(second_key, -3.0, 3.0, shape[1:], jnp.float32)
    magnitude = 0.5 * jnp.exp(fraction * jnp.log(4.0))
    mixing = jax.random.uniform(third_key, (KVEC,), jnp.float32, 0.3, 0.9).reshape(KVEC, 1, 1, 1, 1, 1)
    values = (private * jnp.sqrt(1.0 - mixing * mixing) + mixing * shared[None]) * magnitude
    return values.astype(jnp.float32)


def touch_ends(values, key, least, top_value):
    dims = values.shape
    place = [jax.random.randint(jax.random.fold_in(key, axis), (), 0, dims[axis]) for axis in range(len(dims))]
    values = values.at[tuple(place)].set(least)
    longest = dims.index(max(dims))
    place[longest] = (place[longest] + 1) % dims[longest]
    return values.at[tuple(place)].set(top_value)


def block_levels(rng, extent, pieces, smallest, largest):
    gain = 1.0
    for axis_at, shards_of in pieces:
        heights = jax.random.uniform(jax.random.fold_in(jax.random.fold_in(rng, 6), axis_at), (shards_of,), jnp.float32, smallest / len(pieces), largest / len(pieces))
        gain = gain * jnp.repeat(jnp.exp(heights), extent[axis_at] // shards_of).reshape((-1,) + (1,) * (len(extent) - 1 - axis_at))
    return gain


def normal_values(rng, shape, width, reach, kind=jnp.bfloat16):
    return jnp.clip(width * jax.random.normal(rng, shape, jnp.float32), -reach, reach).astype(kind)


def setup_inputs(seed: int = 0) -> dict:
    streams_of = jax.random.split(jax.random.key(seed), 15)
    return {
        "positions": jnp.clip(1.0 * jax.random.uniform(streams_of[0], (3, GRID_X, GRID_Y, GRID_Z, ATOMS_DEV), jnp.float32) ** block_levels(streams_of[0], (3, GRID_X, GRID_Y, GRID_Z, ATOMS_DEV), ((1, 4), (2, 2), (3, 4)), -0.2, 0.2), 0.0, 1.0),
        "basis": draw_basis(jax.random.fold_in(streams_of[14], 71), 0),
        "neighbours": touch_ends(jax.random.randint(streams_of[2], (GRID_X, GRID_Y, GRID_Z, ATOMS_DEV, NNEI), 0, EXT), jax.random.fold_in(streams_of[2], 1), 0, EXT - 1).astype(jnp.int32),
        "used_count": touch_ends(jax.random.randint(streams_of[3], (GRID_X, GRID_Y, GRID_Z, ATOMS_DEV), NNEI // 3, NNEI + 1), jax.random.fold_in(streams_of[3], 1), NNEI // 3, NNEI).astype(jnp.int32),
        "kinds": touch_ends(jax.random.randint(streams_of[4], (GRID_X, GRID_Y, GRID_Z, ATOMS_DEV), 0, NTYPES), jax.random.fold_in(streams_of[4], 1), 0, NTYPES - 1).astype(jnp.int32),
        "map_x": touch_ends(jax.random.randint(streams_of[5], (GRID_X, GRID_Y, GRID_Z, 2, GHOST), 0, ATOMS_DEV), jax.random.fold_in(streams_of[5], 1), 0, ATOMS_DEV - 1).astype(jnp.int32),
        "map_y": touch_ends(jax.random.randint(streams_of[6], (GRID_X, GRID_Y, GRID_Z, 2, GHOST), 0, ATOMS_DEV + 2 * GHOST), jax.random.fold_in(streams_of[6], 1), 0, (ATOMS_DEV + 2 * GHOST) - 1).astype(jnp.int32),
        "map_z": touch_ends(jax.random.randint(streams_of[7], (GRID_X, GRID_Y, GRID_Z, 2, GHOST), 0, ATOMS_DEV + 4 * GHOST), jax.random.fold_in(streams_of[7], 1), 0, (ATOMS_DEV + 4 * GHOST) - 1).astype(jnp.int32),
        "table": normal_values(streams_of[8], (NTYPES, NBASIS, M1), 1.0, 6.0, jnp.float32),
        "fit_w1": normal_values(streams_of[9], (M1 * M2, FIT), (M1 * M2) ** -0.5, 0.15625, jnp.float32),
        "fit_b1": normal_values(streams_of[10], (FIT,), 0.5, 3.0, jnp.float32),
        "fit_w2": normal_values(streams_of[11], (FIT, FIT), FIT ** -0.5, 0.375, jnp.float32),
        "fit_b2": normal_values(streams_of[12], (FIT,), 0.5, 3.0, jnp.float32),
        "fit_out": normal_values(streams_of[13], (FIT,), FIT ** -0.5, 0.375, jnp.float32),
    }


def site_energy(centre, around, filled, onehot, table, fit_w1, fit_b1, fit_w2, fit_b2, fit_out):
    highest = lax.Precision.HIGHEST
    offsets = around - centre[:, :, None]
    square = lax.optimization_barrier(jnp.sum(offsets * offsets, axis=0))
    radius = jnp.sqrt(square + 0.01)
    smooth = jnp.exp(-square) / radius * filled
    radial = jnp.concatenate([smooth[None], smooth[None] * offsets / radius[None]], axis=0)
    scaled = smooth / (1.0 + smooth)
    levels = table.shape[1]
    centres = jnp.arange(levels, dtype=jnp.float32) / (levels - 1)
    spread = (scaled[:, None, :] - centres[None, :, None]) * (levels - 1)
    profile = jnp.exp(-spread * spread)
    pooled = jnp.einsum('bkn,abn->bka', profile, radial, precision=highest) / around.shape[2]
    tables = jnp.einsum('bt,tkm->bkm', onehot, table, precision=highest)
    environment = jnp.einsum('bkm,bka->bma', tables, pooled, precision=highest)
    descriptor = jnp.einsum('bma,bna->bmn', environment, environment[:, :M2], precision=highest)
    descriptor = descriptor.reshape(descriptor.shape[0], -1)
    first_layer = jnp.tanh(jnp.dot(descriptor, fit_w1, precision=highest) + fit_b1)
    second_layer = jnp.tanh(jnp.dot(first_layer, fit_w2, precision=highest) + fit_b2) + first_layer
    return jnp.sum(jnp.dot(second_layer, fit_out, precision=highest))

def device_hvp(ext_places, ext_tangent, neighbour_ids, counts, species, weights):
    atom_count = neighbour_ids.shape[0]
    block_rows = min(atom_count, 128)
    slots = jnp.arange(neighbour_ids.shape[1], dtype=jnp.int32)
    type_ids = jnp.arange(weights[0].shape[0], dtype=jnp.int32)

    def one_block(counter, summed):
        offset = (counter * block_rows).astype(jnp.int32)
        block_ids = lax.dynamic_slice_in_dim(neighbour_ids, offset, block_rows, 0)
        block_counts = lax.dynamic_slice_in_dim(counts, offset, block_rows, 0)
        block_species = lax.dynamic_slice_in_dim(species, offset, block_rows, 0)
        filled = (slots[None, :] < block_counts[:, None]).astype(jnp.float32)
        onehot = (block_species[:, None] == type_ids[None, :]).astype(jnp.float32)

        def energy(places):
            centre = lax.dynamic_slice_in_dim(places, offset, block_rows, 1)
            return site_energy(centre, places[:, block_ids], filled, onehot, *weights)
        return summed + jax.jvp(jax.grad(energy), (ext_places,), (ext_tangent,))[1]
    zeros = jnp.zeros(ext_places.shape, jnp.float32)
    return lax.fori_loop(0, atom_count // block_rows, one_block, zeros)

def take_rows(values, indices):
    wide = jnp.broadcast_to(indices[None], (values.shape[0],) + indices.shape)
    return jnp.take_along_axis(values, wide, axis=-1)

def extend(places, tangent, maps, axis, coord):
    displace = (jnp.arange(3) == coord).astype(jnp.float32).reshape(3, 1, 1, 1, 1)
    down_places = take_rows(places, maps[..., 0, :])
    up_places = take_rows(places, maps[..., 1, :])
    down_tangent = take_rows(tangent, maps[..., 0, :])
    up_tangent = take_rows(tangent, maps[..., 1, :])
    places = jnp.concatenate([places, jnp.roll(up_places, 1, axis) - displace, jnp.roll(down_places, -1, axis) + displace], axis=-1)
    tangent = jnp.concatenate([tangent, jnp.roll(up_tangent, 1, axis), jnp.roll(down_tangent, -1, axis)], axis=-1)
    return (places, tangent)

def add_one(target, indices, values):
    return target.at[:, indices].add(values)

def add_rows(target, indices, values):
    return jax.vmap(add_one, in_axes=(1, 0, 1), out_axes=1)(target, indices, values)

def reverse_section(contributions, maps, axis, current):
    ghosts = maps.shape[-1]
    bricks = GRID_X * GRID_Y * GRID_Z
    holder = contributions[..., :current]
    lower_part = contributions[..., current:current + ghosts]
    upper_part = contributions[..., current + ghosts:]
    from_below = jnp.roll(upper_part, 1, axis).reshape(3, bricks, ghosts)
    from_above = jnp.roll(lower_part, -1, axis).reshape(3, bricks, ghosts)
    flat = holder.reshape(3, bricks, current)
    flat = add_rows(flat, maps[..., 0, :].reshape(bricks, ghosts), from_below)
    flat = add_rows(flat, maps[..., 1, :].reshape(bricks, ghosts), from_above)
    return flat.reshape(holder.shape)

def reference(positions, basis, neighbours, used_count, kinds, map_x, map_y, map_z, table, fit_w1, fit_b1, fit_w2, fit_b2, fit_out):
    highest = lax.Precision.HIGHEST
    places = positions
    tangent = basis[KVEC - 1]
    places, tangent = extend(places, tangent, map_x, 1, 0)
    places, tangent = extend(places, tangent, map_y, 2, 1)
    places, tangent = extend(places, tangent, map_z, 3, 2)
    bricks = GRID_X * GRID_Y * GRID_Z
    extended = places.shape[-1]
    flat_places = jnp.transpose(places.reshape(3, bricks, extended), (1, 0, 2))
    flat_tangent = jnp.transpose(tangent.reshape(3, bricks, extended), (1, 0, 2))
    flat_ids = neighbours.reshape(bricks, ATOMS_DEV, NNEI)
    flat_counts = used_count.reshape(bricks, ATOMS_DEV)
    flat_species = kinds.reshape(bricks, ATOMS_DEV)
    weights = (table, fit_w1, fit_b1, fit_w2, fit_b2, fit_out)

    def per_brick(packed):
        return device_hvp(packed[0], packed[1], packed[2], packed[3], packed[4], weights)
    products = lax.map(per_brick, (flat_places, flat_tangent, flat_ids, flat_counts, flat_species))
    products = jnp.transpose(products, (1, 0, 2)).reshape(3, GRID_X, GRID_Y, GRID_Z, extended)
    products = reverse_section(products, map_z, 3, ATOMS_DEV + 4 * GHOST)
    products = reverse_section(products, map_y, 2, ATOMS_DEV + 2 * GHOST)
    products = reverse_section(products, map_x, 1, ATOMS_DEV)
    entries = 3 * ATOMS_DEV * bricks
    stored = basis.reshape(KVEC, -1)
    hessian_vec = products.reshape(-1)
    correlations = jnp.dot(stored, hessian_vec, precision=highest) / entries
    residual = hessian_vec - jnp.dot(correlations, stored, precision=highest)
    vector_norm = jnp.sqrt(jnp.sum(residual * residual) / entries + 1e-06)
    next_vector = (residual / vector_norm).reshape(positions.shape)
    return (next_vector, correlations, vector_norm)
```

```python
import functools

import jax
import jax.numpy as jnp
from jax import lax
from jax.experimental import pallas as pl
from jax.experimental.pallas import tpu as pltpu
from jax.sharding import PartitionSpec as P

F32, BF16 = jnp.float32, jnp.bfloat16
HIGHEST = lax.Precision.HIGHEST


def split(x):
    high = x.astype(BF16)
    return high, (x - high.astype(F32)).astype(BF16)


def dot_parts(left, right, dims):
    def one(a, b):
        return lax.dot_general(a, b, (dims, ((), ())), preferred_element_type=F32)

    return one(left[0], right[0]) + (one(left[0], right[1]) + one(left[1], right[0]))


def dot_full(a, b, dims):
    return lax.dot_general(a, b, (dims, ((), ())), precision=HIGHEST, preferred_element_type=F32)


def radial_parts(d, v, mask):
    q = d[0] * d[0] + d[1] * d[1] + d[2] * d[2]
    qd = 2.0 * (d[0] * v[0] + d[1] * v[1] + d[2] * v[2])
    w = 1.0 / (q + 0.01)
    decay = jnp.exp(-q) * mask
    s = decay * jnp.sqrt(w)
    u = decay * w
    s_q = -s * (1.0 + 0.5 * w)
    u_q = -u * (1.0 + w)
    shrink = 1.0 / (1.0 + s)
    t_s = shrink * shrink
    t_q = t_s * s_q
    return q, qd, w, s, u, s_q, u_q, shrink, t_s, t_q


def hvp_kernel(ext_ref, ids_ref, counts_ref, kinds_ref, table_ref, w1_ref, w2_ref, cols_ref, out_ref,
               idt, dv, pool, env, dhi, dlo, gd, genv, gp):
    width, atoms = idt.shape
    types, levels, m1 = table_ref.shape
    m2 = w1_ref.shape[0] // m1
    ext = ext_ref.shape[1]
    banks = ext // 128
    top = float(levels - 1)
    idt[...] = ids_ref[...].T
    pool[...] = jnp.zeros_like(pool)
    counts = counts_ref[...]
    kinds = kinds_ref[...]

    def used(first, rows):
        slot = lax.broadcasted_iota(jnp.int32, (rows, atoms), 0) + first
        return jnp.where(slot < counts, 1.0, 0.0).astype(F32)

    def forward(c, carry):
        first = pl.multiple_of(c * 8, 8)
        idx = idt[pl.ds(first, 8), :]
        lane = jnp.bitwise_and(idx, 127)
        bank = jnp.right_shift(idx, 7)
        fields = []
        for f in range(6):
            got = None
            for b in range(banks):
                row = jnp.broadcast_to(ext_ref[f : f + 1, b * 128 : (b + 1) * 128], (8, 128))
                part = jnp.take_along_axis(row, lane, axis=1, mode="promise_in_bounds")
                got = part if got is None else jnp.where(bank == b, part, got)
            got = got - ext_ref[f : f + 1, :atoms]
            dv[f, pl.ds(first, 8), :] = got
            fields.append(got)
        d, v = fields[:3], fields[3:]
        _, qd, _, s, u, s_q, u_q, shrink, _, t_q = radial_parts(d, v, used(first, 8))
        scaled = s * shrink * top
        r = [s] + [u * e for e in d]
        dr = [s_q * qd] + [u_q * qd * d[e] + u * v[e] for e in range(3)]
        slope = -2.0 * top * t_q * qd
        tr = [slope * e for e in r]
        for k in range(levels):
            y = scaled - float(k)
            phi = jnp.exp(-(y * y))
            psi = y * phi
            for a in range(4):
                pool[a, k] += phi * r[a]
                pool[4 + a, k] += phi * dr[a] + psi * tr[a]
        return carry

    lax.fori_loop(0, width // 8, forward, 0)
    pooled = jnp.concatenate([jnp.sum(pool[a], axis=1) for a in range(8)], axis=1) / width
    kinds8 = jnp.concatenate([kinds] * 8, axis=1)
    chosen = None
    for t in range(types):
        part = dot_full(table_ref[t], pooled, ((0,), (0,)))
        chosen = part if t == 0 else jnp.where(kinds8 == t, part, chosen)
    for a in range(8):
        env[a] = chosen[:, a * atoms : (a + 1) * atoms]
    lead = [env[a, :m2, :] for a in range(8)]

    def describe(m, carry):
        rows = [env[a, pl.ds(m, 1), :] for a in range(8)]
        plain = rows[0] * lead[0]
        moved = rows[4] * lead[0] + rows[0] * lead[4]
        for a in range(1, 4):
            plain += rows[a] * lead[a]
            moved += rows[4 + a] * lead[a] + rows[a] * lead[4 + a]
        place = pl.ds(pl.multiple_of(m * m2, m2), m2)
        for at, value in ((0, plain), (1, moved)):
            high, low = split(value)
            dhi[place, at * atoms : (at + 1) * atoms] = high
            dlo[place, at * atoms : (at + 1) * atoms] = low
        return carry

    lax.fori_loop(0, m1, describe, 0, unroll=4)
    w1 = split(w1_ref[...])
    z1 = dot_parts(w1, (dhi[...], dlo[...]), ((0,), (0,)))
    b1, b2, fo = cols_ref[:, 0:1], cols_ref[:, 1:2], cols_ref[:, 2:3]
    h1 = jnp.tanh(z1[:, :atoms] + b1)
    gate1 = 1.0 - h1 * h1
    dh1 = gate1 * z1[:, atoms:]
    w2 = w2_ref[...]
    z2 = dot_full(w2, jnp.concatenate([h1, dh1], axis=1), ((0,), (0,)))
    t2 = jnp.tanh(z2[:, :atoms] + b2)
    gate2 = 1.0 - t2 * t2
    dt2 = gate2 * z2[:, atoms:]
    gz2 = jnp.concatenate([fo * gate2, fo * (-2.0 * t2 * dt2)], axis=1)
    gh = dot_full(w2, gz2, ((1,), (0,)))
    gh1 = gh[:, :atoms] + fo
    gz1 = jnp.concatenate([gh1 * gate1, gh[:, atoms:] * gate1 - 2.0 * gh1 * h1 * dh1], axis=1)
    gd[...] = dot_parts(w1, split(gz1), ((1,), (0,)))

    def describe_back(m, acc):
        place = pl.ds(pl.multiple_of(m * m2, m2), m2)
        g = gd[place, :atoms]
        dg = gd[place, atoms:]
        out = []
        for a in range(4):
            genv[a, pl.ds(m, 1), :] = jnp.sum(g * lead[a], axis=0, keepdims=True)
            genv[4 + a, pl.ds(m, 1), :] = jnp.sum(
                dg * lead[a] + g * lead[4 + a], axis=0, keepdims=True
            )
        for a in range(4):
            out.append(acc[a] + g * env[a, pl.ds(m, 1), :])
        for a in range(4):
            out.append(
                acc[4 + a]
                + dg * env[a, pl.ds(m, 1), :]
                + g * env[4 + a, pl.ds(m, 1), :]
            )
        return tuple(out)

    acc = lax.fori_loop(0, m1, describe_back, tuple(jnp.zeros((m2, atoms), F32) for _ in range(8)), unroll=2)
    for a in range(8):
        genv[a, :m2, :] += acc[a]
    total = None
    pulled = jnp.concatenate([genv[a] for a in range(8)], axis=1)
    for t in range(types):
        part = dot_full(table_ref[t], jnp.where(kinds8 == t, pulled, 0.0), ((1,), (0,)))
        total = part if total is None else total + part
    total = total / width
    for a in range(8):
        gp[a] = total[:, a * atoms : (a + 1) * atoms]
    low_iota = lax.broadcasted_iota(jnp.int32, (128, atoms), 0)

    def backward(c, carry):
        acc, centre = carry
        first = pl.multiple_of(c * 8, 8)
        d = [dv[f, pl.ds(first, 8), :] for f in range(3)]
        v = [dv[f, pl.ds(first, 8), :] for f in range(3, 6)]
        q, qd, w, s, u, s_q, u_q, shrink, t_s, t_q = radial_parts(d, v, used(first, 8))
        s_qq = -s_q * (1.0 + 0.5 * w) + 0.5 * s * w * w
        u_qq = -u_q * (1.0 + w) + u * w * w
        t_qq = -2.0 * t_s * shrink * s_q * s_q + t_s * s_qq
        scaled = s * shrink * top
        zero = jnp.zeros((8, atoms), F32)
        s0, s1, s2, e0, e1 = ([zero] * 4 for _ in range(5))
        for k in range(levels):
            y = scaled - float(k)
            phi = jnp.exp(-(y * y))
            psi = y * phi
            chi = y * psi
            for a in range(4):
                g = gp[a, k : k + 1, :]
                h = gp[4 + a, k : k + 1, :]
                s0[a] = s0[a] + g * phi
                s1[a] = s1[a] + g * psi
                s2[a] = s2[a] + g * chi
                e0[a] = e0[a] + h * phi
                e1[a] = e1[a] + h * psi
        step = t_q * qd
        val = s0
        val_t = [-2.0 * top * e for e in s1]
        val_tt = [top * top * (4.0 * s2[a] - 2.0 * s0[a]) for a in range(4)]
        dval = [e0[a] + val_t[a] * step for a in range(4)]
        dval_t = [-2.0 * top * e1[a] + val_tt[a] * step for a in range(4)]
        big = val[1] * d[0] + val[2] * d[1] + val[3] * d[2]
        big_t = val_t[1] * d[0] + val_t[2] * d[1] + val_t[3] * d[2]
        dbig = sum(dval[1 + e] * d[e] + val[1 + e] * v[e] for e in range(3))
        dbig_t = sum(dval_t[1 + e] * d[e] + val_t[1 + e] * v[e] for e in range(3))
        kern = t_q * (val_t[0] * s + big_t * u) + val[0] * s_q + big * u_q
        dkern = (
            t_q * (dval_t[0] * s + dbig_t * u)
            + dval[0] * s_q
            + dbig * u_q
            + qd * (
                t_qq * (val_t[0] * s + big_t * u)
                + t_q * (val_t[0] * s_q + big_t * u_q)
                + val[0] * s_qq
                + big * u_qq
            )
        )
        du = u_q * qd
        force = [2.0 * (v[e] * kern + d[e] * dkern) + du * val[1 + e] + u * dval[1 + e] for e in range(3)]
        centre = tuple(centre[e] - force[e] for e in range(3))
        idx = idt[pl.ds(first, 8), :]
        lane = jnp.bitwise_and(idx, 127)
        bank = jnp.right_shift(idx, 7)
        rows = []
        for e in range(3):
            high = force[e].astype(BF16).astype(F32)
            for part in (high, force[e] - high):
                for b in range(banks):
                    rows.append(jnp.where(bank == b, part, 0.0))
        lefts, rights = [], []
        for r in range(8):
            lefts.append(jnp.concatenate([x[r : r + 1, :] for x in rows], axis=0).astype(BF16))
            rights.append(jnp.where(lane[r : r + 1, :] == low_iota, 1.0, 0.0).astype(BF16))
        acc = acc + lax.dot_general(
            jnp.concatenate(lefts, axis=1),
            jnp.concatenate(rights, axis=1),
            (((1,), (1,)), ((), ())),
            preferred_element_type=F32,
        )
        return acc, centre

    out_ref[...] = jnp.zeros_like(out_ref)
    start = (jnp.zeros((6 * banks, 128), F32), tuple(jnp.zeros((8, atoms), F32) for _ in range(3)))
    acc, centre = lax.fori_loop(0, width // 8, backward, start)
    for e in range(3):
        base = 2 * banks * e
        for b in range(banks):
            row = acc[base + b : base + b + 1] + acc[base + banks + b : base + banks + b + 1]
            if b == 0:
                row = row + jnp.sum(centre[e], axis=0, keepdims=True)
            out_ref[e : e + 1, b * 128 : (b + 1) * 128] = row


def device_hvp(fields, neighbour_ids, counts, species, table, w1, w2, columns):
    atoms, width = neighbour_ids.shape
    types, levels, m1 = table.shape
    ext = fields.shape[1]
    m2 = w1.shape[0] // m1
    vmem = pl.BlockSpec(memory_space=pltpu.VMEM)
    return pl.pallas_call(
        hvp_kernel,
        out_shape=jax.ShapeDtypeStruct((8, ext), F32),
        in_specs=[vmem] * 8,
        out_specs=vmem,
        scratch_shapes=[
            pltpu.VMEM((width, atoms), jnp.int32),
            pltpu.VMEM((6, width, atoms), F32),
            pltpu.VMEM((8, levels, 8, atoms), F32),
            pltpu.VMEM((8, m1, atoms), F32),
            pltpu.VMEM((m1 * m2, 2 * atoms), BF16),
            pltpu.VMEM((m1 * m2, 2 * atoms), BF16),
            pltpu.VMEM((m1 * m2, 2 * atoms), F32),
            pltpu.VMEM((8, m1, atoms), F32),
            pltpu.VMEM((8, levels, atoms), F32),
        ],
        compiler_params=pltpu.CompilerParams(vmem_limit_bytes=48 << 20),
        cost_estimate=pl.CostEstimate(flops=1000000000, bytes_accessed=4000000, transcendentals=600000),
        name="hvp",
    )(fields, neighbour_ids, counts.reshape(1, atoms), species.reshape(1, atoms), table, w1, w2, columns)


AXES = ("gx", "gy", "gz")
MESH = pl.DeviceIdType.MESH


def beside(axis):
    peers = lax.axis_size(axis)
    me = lax.axis_index(axis)
    return lax.rem(me + peers - 1, peers), lax.rem(me + 1, peers)


def greet(partners):
    barrier = pltpu.get_barrier_semaphore()
    for axis, peer in partners:
        pl.semaphore_signal(barrier, inc=1, device_id={axis: peer}, device_id_type=MESH)
    pl.semaphore_wait(barrier, len(partners))


def exchange(axis, section, source, landed, send_sem, recv_sem):
    lower, upper = beside(axis)
    copies = []
    for way, peer in ((0, upper), (1, lower)):
        copy = pltpu.make_async_remote_copy(
            src_ref=source,
            dst_ref=landed.at[section, way],
            send_sem=send_sem.at[section, way],
            recv_sem=recv_sem.at[section, way],
            device_id={axis: peer},
            device_id_type=MESH,
        )
        copy.start()
        copies.append(copy)
    for copy in copies:
        copy.wait_recv()
    return copies


def chosen_columns(map_row, columns):
    rows = lax.broadcasted_iota(jnp.int32, (columns, map_row.shape[1]), 0)
    return jnp.where(rows == map_row, 1.0, 0.0).astype(F32)


def halo_kernel(places_ref, tangent_ref, maps_ref, out_ref, sent, landed, send_sem, recv_sem):
    atoms = places_ref.shape[1]
    pair = maps_ref.shape[1]
    greet([(axis, peer) for axis in AXES for peer in beside(axis)])
    out_ref[0:3, :atoms] = places_ref[...]
    out_ref[3:6, :atoms] = tangent_ref[...]
    out_ref[6:8, :] = jnp.zeros((2, out_ref.shape[1]), F32)
    lane = lax.broadcasted_iota(jnp.int32, (8, pair), 1)
    row = lax.broadcasted_iota(jnp.int32, (8, pair), 0)
    early = lane < pair // 2
    waiting = []
    for section, axis in enumerate(AXES):
        current = atoms + section * pair
        onehot = chosen_columns(maps_ref[section : section + 1, :], current)
        sent[section] = dot_full(out_ref[:, :current], onehot, ((1,), (0,)))
        waiting += exchange(axis, section, sent.at[section], landed, send_sem, recv_sem)
        shift = jnp.where(row == section, jnp.where(early, -1.0, 1.0), 0.0)
        fresh = jnp.where(early, landed[section, 0], landed[section, 1]) + shift
        out_ref[:, current : current + pair] = fresh
    for copy in waiting:
        copy.wait_send()


def finish_kernel(w_ref, maps_ref, basis_ref, next_ref, corr_ref, norm_ref,
                  work, landed, stack, parts, send_sem, recv_sem, sum_send, sum_recv):
    stored = basis_ref.shape[1]
    rows = stack.shape[1]
    atoms = basis_ref.shape[2]
    pair = maps_ref.shape[1]
    sizes = [lax.axis_size(axis) for axis in AXES]
    entries = 3 * atoms * sizes[0] * sizes[1] * sizes[2]
    partners = []
    for axis, peers in zip(AXES, sizes):
        me = lax.axis_index(axis)
        partners += [(axis, lax.rem(me + step, peers)) for step in range(1, peers)]
    greet(partners)
    early = lax.broadcasted_iota(jnp.int32, (8, pair), 1) < pair // 2
    work[...] = w_ref[...]
    for c in range(3):
        stack[c] = jnp.zeros((rows, atoms), F32)
        stack[c, :stored, :] = basis_ref[c]
    waiting = []
    for section in (2, 1, 0):
        current = atoms + section * pair
        source = w_ref if section == 2 else work
        waiting += exchange(
            AXES[section], section, source.at[:, current : current + pair], landed, send_sem, recv_sem
        )
        back = jnp.where(early, landed[section, 1], landed[section, 0])
        onehot = chosen_columns(maps_ref[section : section + 1, :], current)
        work[:, :current] = work[:, :current] + dot_full(back, onehot, ((1,), (1,)))
    hv = [work[c : c + 1, :atoms] for c in range(3)]
    local = None
    for c in range(3):
        stack[c, stored : stored + 1, :] = hv[c]
        part = dot_full(stack[c], stack[c], ((1,), (1,)))
        local = part if local is None else local + part
    local = jnp.concatenate([local, jnp.zeros((rows, 128 - rows), F32)], axis=1)
    base = 0
    for at, (axis, peers) in enumerate(zip(AXES, sizes)):
        me = lax.axis_index(axis)
        parts[base + me] = local
        copies = []
        for step in range(1, peers):
            copy = pltpu.make_async_remote_copy(
                src_ref=parts.at[base + me],
                dst_ref=parts.at[base + me],
                send_sem=sum_send.at[base + step],
                recv_sem=sum_recv.at[base + step],
                device_id={axis: lax.rem(me + step, peers)},
                device_id_type=MESH,
            )
            copy.start()
            copies.append(copy)
        for copy in copies:
            copy.wait_recv()
        waiting += copies
        local = parts[base]
        for other in range(1, peers):
            local = local + parts[base + other]
        base += peers
    for copy in waiting:
        copy.wait_send()
    local = local[:, :rows] / entries
    in_row = lax.broadcasted_iota(jnp.int32, (rows, rows), 0)
    in_col = lax.broadcasted_iota(jnp.int32, (rows, rows), 1)
    kept = jnp.logical_and(in_row < stored, in_col < stored)
    column = jnp.where(in_row[:, 0:1] < stored, local[:, stored : stored + 1], 0.0)
    line = local[stored : stored + 1, :]
    line_kept = jnp.where(in_col[0:1] < stored, line, 0.0)
    quad = jnp.where(kept, local * column * line_kept, 0.0)

    def add_up(x):
        return jnp.sum(jnp.sum(x, axis=1, keepdims=True), axis=0, keepdims=True)

    plain = local[stored : stored + 1, stored : stored + 1]
    square = plain - 2.0 * add_up(line_kept * line_kept) + add_up(quad)
    norm = jnp.sqrt(square + 1e-06)
    norm_ref[...] = norm
    corr_ref[...] = line[:, :stored]
    for c in range(3):
        projected = jnp.sum(column * stack[c], axis=0, keepdims=True)
        next_ref[c : c + 1, :] = (hv[c] - projected) / norm


def on_device(positions, basis, neighbours, used_count, kinds, map_x, map_y, map_z,
              table, fit_w1, fit_b1, fit_w2, fit_b2, fit_out):
    atoms = positions.shape[-1]
    stored = basis.shape[0]
    pair = 2 * map_x.shape[-1]
    ext = atoms + 3 * pair
    vectors = jnp.transpose(basis.reshape(stored, 3, atoms), (1, 0, 2))
    maps = jnp.stack([m.reshape(2, -1)[::-1].reshape(-1) for m in (map_x, map_y, map_z)])
    columns = jnp.stack([fit_b1, fit_b2, fit_out], axis=1)
    vmem = pl.BlockSpec(memory_space=pltpu.VMEM)
    fields = pl.pallas_call(
        halo_kernel,
        out_shape=jax.ShapeDtypeStruct((8, ext), F32),
        in_specs=[vmem] * 3,
        out_specs=vmem,
        scratch_shapes=[
            pltpu.VMEM((3, 8, pair), F32),
            pltpu.VMEM((3, 2, 8, pair), F32),
            pltpu.SemaphoreType.DMA((3, 2)),
            pltpu.SemaphoreType.DMA((3, 2)),
        ],
        compiler_params=pltpu.CompilerParams(collective_id=0, has_side_effects=True),
        name="halo",
    )(positions.reshape(3, atoms), vectors[:, stored - 1], maps)
    products = device_hvp(
        fields,
        neighbours.reshape(atoms, -1),
        used_count.reshape(atoms),
        kinds.reshape(atoms),
        table,
        fit_w1,
        fit_w2,
        columns,
    )
    rows = (stored + 8) // 8 * 8
    slots = sum(lax.axis_size(axis) for axis in AXES)
    next_vector, correlations, norm = pl.pallas_call(
        finish_kernel,
        out_shape=(
            jax.ShapeDtypeStruct((3, atoms), F32),
            jax.ShapeDtypeStruct((1, stored), F32),
            jax.ShapeDtypeStruct((1, 1), F32),
        ),
        in_specs=[vmem] * 3,
        out_specs=(vmem,) * 3,
        scratch_shapes=[
            pltpu.VMEM((8, ext), F32),
            pltpu.VMEM((3, 2, 8, pair), F32),
            pltpu.VMEM((3, rows, atoms), F32),
            pltpu.VMEM((slots, rows, 128), F32),
            pltpu.SemaphoreType.DMA((3, 2)),
            pltpu.SemaphoreType.DMA((3, 2)),
            pltpu.SemaphoreType.DMA((slots,)),
            pltpu.SemaphoreType.DMA((slots,)),
        ],
        compiler_params=pltpu.CompilerParams(collective_id=1, has_side_effects=True),
        name="finish",
    )(products, maps, vectors)
    return next_vector.reshape(positions.shape), correlations.reshape(stored), norm.reshape(())


def solution(mesh):
    placed = (
        P(None, "gx", "gy", "gz", None),
        P(None, None, "gx", "gy", "gz", None),
        P("gx", "gy", "gz", None, None),
        P("gx", "gy", "gz", None),
        P("gx", "gy", "gz", None),
        P("gx", "gy", "gz", None, None),
        P("gx", "gy", "gz", None, None),
        P("gx", "gy", "gz", None, None),
        P(),
        P(),
        P(),
        P(),
        P(),
        P(),
    )
    return jax.shard_map(
        on_device,
        mesh=mesh,
        in_specs=placed,
        out_specs=(P(None, "gx", "gy", "gz", None), P(), P()),
        check_vma=False,
    )
```

```python
import functools

import jax
import jax.numpy as jnp
from jax import lax
from jax.experimental import pallas as pl
from jax.experimental.pallas import tpu as pltpu
from jax.sharding import PartitionSpec as P

F32, BF16 = jnp.float32, jnp.bfloat16
HIGHEST = lax.Precision.HIGHEST


def split(x):
    high = x.astype(BF16)
    return high, (x - high.astype(F32)).astype(BF16)


def dot_parts(left, right, dims):
    def one(a, b):
        return lax.dot_general(a, b, (dims, ((), ())), preferred_element_type=F32)

    return one(left[0], right[0]) + (one(left[0], right[1]) + one(left[1], right[0]))


def dot_full(a, b, dims):
    return lax.dot_general(a, b, (dims, ((), ())), precision=HIGHEST, preferred_element_type=F32)


def radial_parts(d, v, mask):
    q = d[0] * d[0] + d[1] * d[1] + d[2] * d[2]
    qd = 2.0 * (d[0] * v[0] + d[1] * v[1] + d[2] * v[2])
    w = 1.0 / (q + 0.01)
    decay = jnp.exp(-q) * mask
    s = decay * jnp.sqrt(w)
    u = decay * w
    s_q = -s * (1.0 + 0.5 * w)
    u_q = -u * (1.0 + w)
    shrink = 1.0 / (1.0 + s)
    t_s = shrink * shrink
    t_q = t_s * s_q
    return q, qd, w, s, u, s_q, u_q, shrink, t_s, t_q


def hvp_kernel(ext_ref, ids_ref, counts_ref, kinds_ref, table_ref, w1_ref, w2_ref, b1_ref, b2_ref, fo_ref, out_ref,
               idt, dv, pool, env, dhi, dlo, gd, genv, gp):
    width, atoms = idt.shape
    types, levels, m1 = table_ref.shape
    m2 = w1_ref.shape[1] // m1
    ext = ext_ref.shape[1]
    banks = ext // 128
    top = float(levels - 1)
    idt[...] = ids_ref[...].T
    pool[...] = jnp.zeros_like(pool)
    counts = counts_ref[...]
    kinds = kinds_ref[...]

    def used(first, rows):
        slot = lax.broadcasted_iota(jnp.int32, (rows, atoms), 0) + first
        return jnp.where(slot < counts, 1.0, 0.0).astype(F32)

    def forward(c, carry):
        first = pl.multiple_of(c * 8, 8)
        idx = idt[pl.ds(first, 8), :]
        lane = jnp.bitwise_and(idx, 127)
        bank = jnp.right_shift(idx, 7)
        fields = []
        for f in range(6):
            got = None
            for b in range(banks):
                row = jnp.broadcast_to(ext_ref[f : f + 1, b * 128 : (b + 1) * 128], (8, 128))
                part = jnp.take_along_axis(row, lane, axis=1, mode="promise_in_bounds")
                got = part if got is None else jnp.where(bank == b, part, got)
            got = got - ext_ref[f : f + 1, :atoms]
            dv[f, pl.ds(first, 8), :] = got
            fields.append(got)
        d, v = fields[:3], fields[3:]
        _, qd, _, s, u, s_q, u_q, shrink, _, t_q = radial_parts(d, v, used(first, 8))
        scaled = s * shrink * top
        r = [s] + [u * e for e in d]
        dr = [s_q * qd] + [u_q * qd * d[e] + u * v[e] for e in range(3)]
        slope = -2.0 * top * t_q * qd
        tr = [slope * e for e in r]
        for k in range(levels):
            y = scaled - float(k)
            phi = jnp.exp(-(y * y))
            psi = y * phi
            for a in range(4):
                pool[a, k] += phi * r[a]
                pool[4 + a, k] += phi * dr[a] + psi * tr[a]
        return carry

    lax.fori_loop(0, width // 8, forward, 0)
    pooled = jnp.concatenate([jnp.sum(pool[a], axis=1) for a in range(8)], axis=1) / width
    kinds8 = jnp.concatenate([kinds] * 8, axis=1)
    chosen = None
    for t in range(types):
        part = dot_full(table_ref[t], pooled, ((0,), (0,)))
        chosen = part if t == 0 else jnp.where(kinds8 == t, part, chosen)
    for a in range(8):
        env[a] = chosen[:, a * atoms : (a + 1) * atoms]
    lead = [env[a, :m2, :] for a in range(8)]

    def describe(m, carry):
        rows = [env[a, pl.ds(m, 1), :] for a in range(8)]
        plain = rows[0] * lead[0]
        moved = rows[4] * lead[0] + rows[0] * lead[4]
        for a in range(1, 4):
            plain += rows[a] * lead[a]
            moved += rows[4 + a] * lead[a] + rows[a] * lead[4 + a]
        place = pl.ds(pl.multiple_of(m * m2, m2), m2)
        for at, value in ((0, plain), (1, moved)):
            high, low = split(value)
            dhi[place, at * atoms : (at + 1) * atoms] = high
            dlo[place, at * atoms : (at + 1) * atoms] = low
        return carry

    lax.fori_loop(0, m1, describe, 0, unroll=4)
    w1 = split(w1_ref[...])
    z1 = dot_parts(w1, (dhi[...], dlo[...]), ((1,), (0,)))
    fit = b1_ref.shape[1]
    lines = jnp.concatenate([b1_ref[...], b2_ref[...], fo_ref[...], jnp.zeros((5, fit), F32)], axis=0)
    same = lax.broadcasted_iota(jnp.int32, (8, 8), 0) == lax.broadcasted_iota(jnp.int32, (8, 8), 1)
    cols = dot_full(lines, jnp.where(same, 1.0, 0.0).astype(F32), ((0,), (0,)))
    b1, b2, fo = cols[:, 0:1], cols[:, 1:2], cols[:, 2:3]
    h1 = jnp.tanh(z1[:, :atoms] + b1)
    gate1 = 1.0 - h1 * h1
    dh1 = gate1 * z1[:, atoms:]
    w2 = w2_ref[...]
    z2 = dot_full(w2, jnp.concatenate([h1, dh1], axis=1), ((0,), (0,)))
    t2 = jnp.tanh(z2[:, :atoms] + b2)
    gate2 = 1.0 - t2 * t2
    dt2 = gate2 * z2[:, atoms:]
    gz2 = jnp.concatenate([fo * gate2, fo * (-2.0 * t2 * dt2)], axis=1)
    gh = dot_full(w2, gz2, ((1,), (0,)))
    gh1 = gh[:, :atoms] + fo
    gz1 = jnp.concatenate([gh1 * gate1, gh[:, atoms:] * gate1 - 2.0 * gh1 * h1 * dh1], axis=1)
    gd[...] = dot_parts(w1, split(gz1), ((0,), (0,)))

    def describe_back(m, acc):
        place = pl.ds(pl.multiple_of(m * m2, m2), m2)
        g = gd[place, :atoms]
        dg = gd[place, atoms:]
        out = []
        for a in range(4):
            genv[a, pl.ds(m, 1), :] = jnp.sum(g * lead[a], axis=0, keepdims=True)
            genv[4 + a, pl.ds(m, 1), :] = jnp.sum(
                dg * lead[a] + g * lead[4 + a], axis=0, keepdims=True
            )
        for a in range(4):
            out.append(acc[a] + g * env[a, pl.ds(m, 1), :])
        for a in range(4):
            out.append(
                acc[4 + a]
                + dg * env[a, pl.ds(m, 1), :]
                + g * env[4 + a, pl.ds(m, 1), :]
            )
        return tuple(out)

    acc = lax.fori_loop(0, m1, describe_back, tuple(jnp.zeros((m2, atoms), F32) for _ in range(8)), unroll=2)
    for a in range(8):
        genv[a, :m2, :] += acc[a]
    total = None
    pulled = jnp.concatenate([genv[a] for a in range(8)], axis=1)
    for t in range(types):
        part = dot_full(table_ref[t], jnp.where(kinds8 == t, pulled, 0.0), ((1,), (0,)))
        total = part if total is None else total + part
    total = total / width
    for a in range(8):
        gp[a] = total[:, a * atoms : (a + 1) * atoms]
    low_iota = lax.broadcasted_iota(jnp.int32, (128, atoms), 0)

    def backward(c, carry):
        acc, centre = carry
        first = pl.multiple_of(c * 8, 8)
        d = [dv[f, pl.ds(first, 8), :] for f in range(3)]
        v = [dv[f, pl.ds(first, 8), :] for f in range(3, 6)]
        q, qd, w, s, u, s_q, u_q, shrink, t_s, t_q = radial_parts(d, v, used(first, 8))
        s_qq = -s_q * (1.0 + 0.5 * w) + 0.5 * s * w * w
        u_qq = -u_q * (1.0 + w) + u * w * w
        t_qq = -2.0 * t_s * shrink * s_q * s_q + t_s * s_qq
        scaled = s * shrink * top
        zero = jnp.zeros((8, atoms), F32)
        s0, s1, s2, e0, e1 = ([zero] * 4 for _ in range(5))
        for k in range(levels):
            y = scaled - float(k)
            phi = jnp.exp(-(y * y))
            psi = y * phi
            chi = y * psi
            for a in range(4):
                g = gp[a, k : k + 1, :]
                h = gp[4 + a, k : k + 1, :]
                s0[a] = s0[a] + g * phi
                s1[a] = s1[a] + g * psi
                s2[a] = s2[a] + g * chi
                e0[a] = e0[a] + h * phi
                e1[a] = e1[a] + h * psi
        step = t_q * qd
        val = s0
        val_t = [-2.0 * top * e for e in s1]
        val_tt = [top * top * (4.0 * s2[a] - 2.0 * s0[a]) for a in range(4)]
        dval = [e0[a] + val_t[a] * step for a in range(4)]
        dval_t = [-2.0 * top * e1[a] + val_tt[a] * step for a in range(4)]
        big = val[1] * d[0] + val[2] * d[1] + val[3] * d[2]
        big_t = val_t[1] * d[0] + val_t[2] * d[1] + val_t[3] * d[2]
        dbig = sum(dval[1 + e] * d[e] + val[1 + e] * v[e] for e in range(3))
        dbig_t = sum(dval_t[1 + e] * d[e] + val_t[1 + e] * v[e] for e in range(3))
        kern = t_q * (val_t[0] * s + big_t * u) + val[0] * s_q + big * u_q
        dkern = (
            t_q * (dval_t[0] * s + dbig_t * u)
            + dval[0] * s_q
            + dbig * u_q
            + qd * (
                t_qq * (val_t[0] * s + big_t * u)
                + t_q * (val_t[0] * s_q + big_t * u_q)
                + val[0] * s_qq
                + big * u_qq
            )
        )
        du = u_q * qd
        force = [2.0 * (v[e] * kern + d[e] * dkern) + du * val[1 + e] + u * dval[1 + e] for e in range(3)]
        centre = tuple(centre[e] - force[e] for e in range(3))
        idx = idt[pl.ds(first, 8), :]
        lane = jnp.bitwise_and(idx, 127)
        bank = jnp.right_shift(idx, 7)
        rows = []
        for e in range(3):
            high = force[e].astype(BF16).astype(F32)
            for part in (high, force[e] - high):
                for b in range(banks):
                    rows.append(jnp.where(bank == b, part, 0.0))
        lefts, rights = [], []
        for r in range(8):
            lefts.append(jnp.concatenate([x[r : r + 1, :] for x in rows], axis=0).astype(BF16))
            rights.append(jnp.where(lane[r : r + 1, :] == low_iota, 1.0, 0.0).astype(BF16))
        acc = acc + lax.dot_general(
            jnp.concatenate(lefts, axis=1),
            jnp.concatenate(rights, axis=1),
            (((1,), (1,)), ((), ())),
            preferred_element_type=F32,
        )
        return acc, centre

    out_ref[...] = jnp.zeros_like(out_ref)
    start = (jnp.zeros((6 * banks, 128), F32), tuple(jnp.zeros((8, atoms), F32) for _ in range(3)))
    acc, centre = lax.fori_loop(0, width // 8, backward, start)
    for e in range(3):
        base = 2 * banks * e
        for b in range(banks):
            row = acc[base + b : base + b + 1] + acc[base + banks + b : base + banks + b + 1]
            if b == 0:
                row = row + jnp.sum(centre[e], axis=0, keepdims=True)
            out_ref[e : e + 1, b * 128 : (b + 1) * 128] = row


def device_hvp(fields, neighbour_ids, counts, species, table, w1, w2, b1, b2, fo):
    atoms, width = neighbour_ids.shape
    types, levels, m1 = table.shape
    ext = fields.shape[1]
    m2 = w1.shape[1] // m1
    vmem = pl.BlockSpec(memory_space=pltpu.VMEM)
    return pl.pallas_call(
        hvp_kernel,
        out_shape=jax.ShapeDtypeStruct((8, ext), F32),
        in_specs=[vmem] * 10,
        out_specs=vmem,
        scratch_shapes=[
            pltpu.VMEM((width, atoms), jnp.int32),
            pltpu.VMEM((6, width, atoms), F32),
            pltpu.VMEM((8, levels, 8, atoms), F32),
            pltpu.VMEM((8, m1, atoms), F32),
            pltpu.VMEM((m1 * m2, 2 * atoms), BF16),
            pltpu.VMEM((m1 * m2, 2 * atoms), BF16),
            pltpu.VMEM((m1 * m2, 2 * atoms), F32),
            pltpu.VMEM((8, m1, atoms), F32),
            pltpu.VMEM((8, levels, atoms), F32),
        ],
        compiler_params=pltpu.CompilerParams(vmem_limit_bytes=48 << 20),
        cost_estimate=pl.CostEstimate(flops=1000000000, bytes_accessed=4000000, transcendentals=600000),
        name="hvp",
    )(fields, neighbour_ids, counts.reshape(1, atoms), species.reshape(1, atoms), table, w1, w2, b1[None], b2[None], fo[None])


AXES = ("gx", "gy", "gz")
MESH = pl.DeviceIdType.MESH


def beside(axis):
    peers = lax.axis_size(axis)
    me = lax.axis_index(axis)
    return lax.rem(me + peers - 1, peers), lax.rem(me + 1, peers)


def greet(partners):
    barrier = pltpu.get_barrier_semaphore()
    for axis, peer in partners:
        pl.semaphore_signal(barrier, inc=1, device_id={axis: peer}, device_id_type=MESH)
    return lambda: pl.semaphore_wait(barrier, len(partners))


def three_parts(x):
    high = x.astype(BF16)
    rest = x - high.astype(F32)
    middle = rest.astype(BF16)
    low = (rest - middle.astype(F32)).astype(BF16)
    return jnp.concatenate([high.astype(F32), middle.astype(F32), low.astype(F32)], axis=0).astype(BF16)


def select_dot(x, onehot, dims):
    n = x.shape[0]
    out = lax.dot_general(three_parts(x), onehot, (dims, ((), ())), preferred_element_type=F32)
    return (out[:n] + out[n : 2 * n]) + out[2 * n :]


def exchange(axis, section, source, landed, send_sem, recv_sem):
    lower, upper = beside(axis)
    copies = []
    for way, peer in ((0, upper), (1, lower)):
        copy = pltpu.make_async_remote_copy(
            src_ref=source,
            dst_ref=landed.at[section, way],
            send_sem=send_sem.at[section, way],
            recv_sem=recv_sem.at[section, way],
            device_id={axis: peer},
            device_id_type=MESH,
        )
        copy.start()
        copies.append(copy)
    for copy in copies:
        copy.wait_recv()
    return copies


def chosen_columns(map_ref, columns):
    map_row = jnp.concatenate([map_ref[1:2, :], map_ref[0:1, :]], axis=1)
    rows = lax.broadcasted_iota(jnp.int32, (columns, map_row.shape[1]), 0)
    return jnp.where(rows == map_row, 1.0, 0.0).astype(BF16)


def halo_kernel(places_ref, basis_ref, map_x_ref, map_y_ref, map_z_ref, out_ref,
                sent, landed, send_sem, recv_sem):
    atoms = places_ref.shape[2]
    maps = (map_x_ref, map_y_ref, map_z_ref)
    pair = 2 * map_x_ref.shape[1]
    arrived = greet([(axis, peer) for axis in AXES for peer in beside(axis)])
    last = basis_ref.shape[0] - 1
    for c in range(3):
        out_ref[c : c + 1, :atoms] = places_ref[c]
        out_ref[3 + c : 4 + c, :atoms] = basis_ref[last, c]
    out_ref[6:8, :] = jnp.zeros((2, out_ref.shape[1]), F32)
    lane = lax.broadcasted_iota(jnp.int32, (8, pair), 1)
    row = lax.broadcasted_iota(jnp.int32, (8, pair), 0)
    early = lane < pair // 2
    waiting = []
    onehots = [chosen_columns(maps[section], atoms + section * pair) for section in range(3)]
    for section, axis in enumerate(AXES):
        current = atoms + section * pair
        sent[section] = select_dot(out_ref[:, :current], onehots[section], ((1,), (0,)))
        if section == 0:
            arrived()
        waiting += exchange(axis, section, sent.at[section], landed, send_sem, recv_sem)
        shift = jnp.where(row == section, jnp.where(early, -1.0, 1.0), 0.0)
        fresh = jnp.where(early, landed[section, 0], landed[section, 1]) + shift
        out_ref[:, current : current + pair] = fresh
    for copy in waiting:
        copy.wait_send()


def finish_kernel(w_ref, map_x_ref, map_y_ref, map_z_ref, basis_ref, next_ref, corr_ref, norm_ref,
                  work, landed, stack, parts, send_sem, recv_sem, sum_send, sum_recv):
    stored = basis_ref.shape[0]
    rows = stack.shape[0]
    atoms = basis_ref.shape[3]
    maps = (map_x_ref, map_y_ref, map_z_ref)
    pair = 2 * map_x_ref.shape[1]
    sizes = [lax.axis_size(axis) for axis in AXES]
    entries = 3 * atoms * sizes[0] * sizes[1] * sizes[2]
    partners = []
    for axis, peers in zip(AXES, sizes):
        me = lax.axis_index(axis)
        partners += [(axis, lax.rem(me + step, peers)) for step in range(1, peers)]
    arrived = greet(partners)
    early = lax.broadcasted_iota(jnp.int32, (8, pair), 1) < pair // 2
    work[...] = w_ref[...]
    stack[...] = jnp.zeros_like(stack)
    for k in range(stored):
        for c in range(3):
            stack[k : k + 1, c * atoms : (c + 1) * atoms] = basis_ref[k, c]
    waiting = []
    onehots = [chosen_columns(maps[section], atoms + section * pair) for section in range(3)]
    arrived()
    for section in (2, 1, 0):
        current = atoms + section * pair
        source = w_ref if section == 2 else work
        waiting += exchange(
            AXES[section], section, source.at[:, current : current + pair], landed, send_sem, recv_sem
        )
        back = jnp.where(early, landed[section, 1], landed[section, 0])
        work[:, :current] = work[:, :current] + select_dot(back, onehots[section], ((1,), (1,)))
    hv = [work[c : c + 1, :atoms] for c in range(3)]
    for c in range(3):
        stack[stored : stored + 1, c * atoms : (c + 1) * atoms] = hv[c]
    local = dot_full(stack[...], stack[...], ((1,), (1,)))
    local = jnp.concatenate([local[r : r + 8] for r in range(0, rows, 8)], axis=1)
    base = 0
    for at, (axis, peers) in enumerate(zip(AXES, sizes)):
        me = lax.axis_index(axis)
        parts[base + me] = local
        copies = []
        for step in range(1, peers):
            copy = pltpu.make_async_remote_copy(
                src_ref=parts.at[base + me],
                dst_ref=parts.at[base + me],
                send_sem=sum_send.at[base + step],
                recv_sem=sum_recv.at[base + step],
                device_id={axis: lax.rem(me + step, peers)},
                device_id_type=MESH,
            )
            copy.start()
            copies.append(copy)
        for copy in copies:
            copy.wait_recv()
        waiting += copies
        local = parts[base]
        for other in range(1, peers):
            local = local + parts[base + other]
        base += peers
    for copy in waiting:
        copy.wait_send()
    local = jnp.concatenate([local[:, r : r + rows] for r in range(0, rows * rows // 8, rows)], axis=0) / entries
    in_row = lax.broadcasted_iota(jnp.int32, (rows, rows), 0)
    in_col = lax.broadcasted_iota(jnp.int32, (rows, rows), 1)
    kept = jnp.logical_and(in_row < stored, in_col < stored)
    column = jnp.where(in_row[:, 0:1] < stored, local[:, stored : stored + 1], 0.0)
    line = local[stored : stored + 1, :]
    line_kept = jnp.where(in_col[0:1] < stored, line, 0.0)
    quad = jnp.where(kept, local * column * line_kept, 0.0)

    def add_up(x):
        return jnp.sum(jnp.sum(x, axis=1, keepdims=True), axis=0, keepdims=True)

    plain = local[stored : stored + 1, stored : stored + 1]
    square = plain - 2.0 * add_up(line_kept * line_kept) + add_up(quad)
    norm = jnp.sqrt(square + 1e-06)
    norm_ref[...] = norm
    corr_ref[...] = line[:, :stored]
    for c in range(3):
        projected = jnp.sum(column * stack[:, c * atoms : (c + 1) * atoms], axis=0, keepdims=True)
        next_ref[c] = (hv[c] - projected) / norm


def on_device(positions, basis, neighbours, used_count, kinds, map_x, map_y, map_z,
              table, fit_w1, fit_b1, fit_w2, fit_b2, fit_out):
    atoms = positions.shape[-1]
    stored = basis.shape[0]
    pair = 2 * map_x.shape[-1]
    ext = atoms + 3 * pair
    vectors = basis.reshape(stored, 3, 1, atoms)
    maps = tuple(m.reshape(2, -1) for m in (map_x, map_y, map_z))
    vmem = pl.BlockSpec(memory_space=pltpu.VMEM)
    fields = pl.pallas_call(
        halo_kernel,
        out_shape=jax.ShapeDtypeStruct((8, ext), F32),
        in_specs=[vmem] * 5,
        out_specs=vmem,
        scratch_shapes=[
            pltpu.VMEM((3, 8, pair), F32),
            pltpu.VMEM((3, 2, 8, pair), F32),
            pltpu.SemaphoreType.DMA((3, 2)),
            pltpu.SemaphoreType.DMA((3, 2)),
        ],
        compiler_params=pltpu.CompilerParams(collective_id=0, has_side_effects=True),
        cost_estimate=pl.CostEstimate(flops=1000000000, bytes_accessed=4000000, transcendentals=0),
        name="halo",
    )(positions.reshape(3, 1, atoms), vectors, *maps)
    products = device_hvp(
        fields,
        neighbours.reshape(atoms, -1),
        used_count.reshape(atoms),
        kinds.reshape(atoms),
        table,
        fit_w1.T,
        fit_w2,
        fit_b1,
        fit_b2,
        fit_out,
    )
    rows = (stored + 8) // 8 * 8
    slots = sum(lax.axis_size(axis) for axis in AXES)
    next_vector, correlations, norm = pl.pallas_call(
        finish_kernel,
        out_shape=(
            jax.ShapeDtypeStruct((3, 1, atoms), F32),
            jax.ShapeDtypeStruct((1, stored), F32),
            jax.ShapeDtypeStruct((1, 1), F32),
        ),
        in_specs=[vmem] * 5,
        out_specs=(vmem,) * 3,
        scratch_shapes=[
            pltpu.VMEM((8, ext), F32),
            pltpu.VMEM((3, 2, 8, pair), F32),
            pltpu.VMEM((rows, 3 * atoms), F32),
            pltpu.VMEM((slots, 8, rows * rows // 8), F32),
            pltpu.SemaphoreType.DMA((3, 2)),
            pltpu.SemaphoreType.DMA((3, 2)),
            pltpu.SemaphoreType.DMA((slots,)),
            pltpu.SemaphoreType.DMA((slots,)),
        ],
        compiler_params=pltpu.CompilerParams(collective_id=1, has_side_effects=True),
        name="finish",
    )(products, *maps, vectors)
    return next_vector.reshape(positions.shape), correlations.reshape(stored), norm.reshape(())


def solution(mesh):
    placed = (
        P(None, "gx", "gy", "gz", None),
        P(None, None, "gx", "gy", "gz", None),
        P("gx", "gy", "gz", None, None),
        P("gx", "gy", "gz", None),
        P("gx", "gy", "gz", None),
        P("gx", "gy", "gz", None, None),
        P("gx", "gy", "gz", None, None),
        P("gx", "gy", "gz", None, None),
        P(),
        P(),
        P(),
        P(),
        P(),
        P(),
    )
    return jax.shard_map(
        on_device,
        mesh=mesh,
        in_specs=placed,
        out_specs=(P(None, "gx", "gy", "gz", None), P(), P()),
        check_vma=False,
    )
```
